128 devices in a mesh: leaf: 128 (over x, y, z, core).
Axes of the slice: x: 4, y: 4, z: 4, core: 2. Of those that a mesh axis runs over, the one named last changes fastest.
Arguments:
- probes: float32 [131072, 1024], P('leaf'), may hold values from -6 to 6
- leaf_basis: float32 [256, 512, 64], P('leaf'), may hold values from -0.25 to 0.25
- leaf_transfer: float32 [256, 64, 64], P('leaf'), may hold values from -0.75 to 0.75
- cluster_transfer: float32 [64, 64, 64], replicated, may hold values from -0.75 to 0.75
- couple_one: float32 [512, 64, 64], P('leaf'), may hold values from -0.75 to 0.75
- pairs_one: int32 [512], P('leaf'), may hold values from 0 to 63, as said below
- count_one: int32 [64], replicated, may hold values from 0 to 8
- couple_two: float32 [128, 64, 64], P('leaf'), may hold values from -0.75 to 0.75
- pairs_two: int32 [128], P('leaf'), may hold values from 0 to 15, as said below
- count_two: int32 [16], replicated, may hold values from 0 to 8
- near_blocks: float32 [256, 3, 512, 512], P('leaf'), may hold values from -0.15625 to 0.15625
- near_list: int32 [256, 3], P('leaf'), may hold values from 0 to 255, as said below
Outputs:
- kernel_times: float32 [131072, 1024], P('leaf')
The draws below stay inside these ranges and needn't reach their ends.
Inputs may be any that keep to these rules, and one draw needn't show every extreme that they name: `pairs_one`: for slots k < count_one[c], the partners of cluster c are distinct clusters j with |j - c| >= 2 and |j // 4 - c // 4| <= 1; the other slots hold c itself. `pairs_two`: for slots k < count_two[q], the partners of cluster q are distinct clusters j with |j - q| >= 2 and |j // 4 - q // 4| <= 1; the other slots hold q itself. near_list[i, 0] is i, and every entry of row i lies within i - 2 to i + 2.
All inputs are finite; a program needn't handle non-finite values.
Results may differ from the reference program's by a relative error of at most 0.000086.
Values sent between devices are 32-bit elements; how exact they have to be, the bound alone decides.
No kernel may reach another device: no remote copies, remote signals or barrier semaphores. Data moves between devices by JAX's collectives and lax.ppermute only.
A program may use at most 128 MiB of HBM per device.

```python
import jax
import jax.numpy as jnp
from jax import lax

LEAF = 512
RANK = 64
PROBES = 1024
NEAR = 3
COUPLE_SLOTS = 8
LEAVES = 256
POINTS = 131072
CLUSTERS_ONE = 64
CLUSTERS_TWO = 16


offset_table = (-7, -6, -5, -4, -3, -2, 2, 3, 4, 5, 6, 7)


near_table = (-2, -1, 1, 2)


def partner_table(key, clusters):
    centers = jnp.arange(clusters, dtype=jnp.int32)[:, None]
    offsets = jnp.array(offset_table, jnp.int32)[None, :]
    candidate = centers + offsets
    usable = (candidate >= 0) & (candidate < clusters) & (jnp.abs(jnp.floor_divide(candidate, 4) - centers // 4) <= 1)
    scores = jax.random.randint(jax.random.fold_in(key, 1), (clusters, 12), 0, 1024) * 16 + jnp.arange(12, dtype=jnp.int32)[None, :]
    scores = jnp.where(usable, scores, scores + 65536)
    ranking = jnp.argsort(scores, axis=1, stable=True)
    chosen = jnp.take_along_axis(candidate, ranking, axis=1)[:, :COUPLE_SLOTS]
    usable_count = jnp.minimum(jnp.sum(usable.astype(jnp.int32), axis=1), COUPLE_SLOTS)
    tie_break = jax.random.randint(jax.random.fold_in(key, 4), (clusters,), 0, 1024)
    busiest = jnp.argmax(usable_count * 1024 + tie_break).astype(jnp.int32)
    loaded = jax.random.randint(jax.random.fold_in(key, 2), (clusters,), 0, 4) == 0
    loaded = loaded | (jnp.arange(clusters, dtype=jnp.int32) == busiest)
    spread = jax.random.randint(jax.random.fold_in(key, 3), (clusters,), 0, 1 << 20) % (usable_count + 1)
    counts = jnp.where(loaded, usable_count, spread)
    slot_index = jnp.arange(COUPLE_SLOTS, dtype=jnp.int32)[None, :]
    partner_ids = jnp.where(slot_index < counts[:, None], chosen, centers)
    return (partner_ids.reshape(-1).astype(jnp.int32), counts.astype(jnp.int32))


def draw_pairs_one(key, part):
    return partner_table(jax.random.fold_in(key, 11), CLUSTERS_ONE)[0]


def draw_count_one(key, part):
    return partner_table(jax.random.fold_in(key, 11), CLUSTERS_ONE)[1]


def draw_pairs_two(key, part):
    return partner_table(jax.random.fold_in(key, 22), CLUSTERS_TWO)[0]


def draw_count_two(key, part):
    return partner_table(jax.random.fold_in(key, 22), CLUSTERS_TWO)[1]


def draw_near_list(key, part):
    leaf_ids = jnp.arange(LEAVES, dtype=jnp.int32)[:, None]
    scores = jax.random.randint(jax.random.fold_in(key, 5), (LEAVES, 4), 0, 1024) * 8 + jnp.arange(4, dtype=jnp.int32)[None, :]
    ranking = jnp.argsort(scores, axis=1, stable=True)[:, :NEAR - 1]
    offsets = jnp.take(jnp.array(near_table, jnp.int32), ranking)
    target = leaf_ids + offsets
    target = jnp.where((target < 0) | (target >= LEAVES), leaf_ids - offsets, target)
    return jnp.concatenate([leaf_ids, target], axis=1).astype(jnp.int32)


def levels(stream_key, dims, cuts, smallest, top_value):
    def one(axis_at, parts):
        steps = jax.random.uniform(jax.random.fold_in(jax.random.fold_in(stream_key, 6), axis_at), (parts,), jnp.float32, smallest / len(cuts), top_value / len(cuts))
        return jnp.repeat(jnp.exp(steps), dims[axis_at] // parts).reshape((-1,) + (1,) * (len(dims) - axis_at - 1))

    factor_of = one(*cuts[0])
    for cut in cuts[1:]:
        factor_of = factor_of * one(*cut)
    return factor_of


def scatter_about(key, shape, scale, bound, shards=(), held_as=jnp.bfloat16):
    factor_of = levels(key, shape, shards, -0.22, 0.18) if shards else 1.0
    entries = jax.random.normal(key, shape, jnp.float32) * scale * factor_of
    return jnp.minimum(jnp.maximum(entries, -bound), bound).astype(held_as)


def setup_inputs(seed: int = 0) -> dict:
    arg_keys = jax.random.split(jax.random.key(seed), 13)
    probes = scatter_about(arg_keys[0], (POINTS, PROBES), 1.0, 6.0, ((0, 128),), jnp.float32)
    leaf_basis = scatter_about(arg_keys[1], (LEAVES, LEAF, RANK), LEAF ** -0.5, 0.25, ((0, 128),), jnp.float32)
    leaf_transfer = scatter_about(arg_keys[2], (LEAVES, RANK, RANK), RANK ** -0.5, 0.75, ((0, 128),), jnp.float32)
    cluster_transfer = scatter_about(arg_keys[3], (CLUSTERS_ONE, RANK, RANK), RANK ** -0.5, 0.75, (), jnp.float32)
    couple_one = scatter_about(arg_keys[4], (CLUSTERS_ONE * COUPLE_SLOTS, RANK, RANK), RANK ** -0.5, 0.75, ((0, 128),), jnp.float32)
    pairs_one = draw_pairs_one(jax.random.fold_in(arg_keys[12], 71), 0)
    count_one = draw_count_one(jax.random.fold_in(arg_keys[12], 71), 0)
    couple_two = scatter_about(arg_keys[7], (CLUSTERS_TWO * COUPLE_SLOTS, RANK, RANK), RANK ** -0.5, 0.75, ((0, 128),), jnp.float32)
    pairs_two = draw_pairs_two(jax.random.fold_in(arg_keys[12], 71), 0)
    count_two = draw_count_two(jax.random.fold_in(arg_keys[12], 71), 0)
    near_blocks = scatter_about(arg_keys[10], (LEAVES, NEAR, LEAF, LEAF), (LEAF * NEAR) ** -0.5, 0.15625, ((0, 128),), jnp.float32)
    near_list = draw_near_list(jax.random.fold_in(arg_keys[12], 71), 0)
    return dict(probes=probes, leaf_basis=leaf_basis, leaf_transfer=leaf_transfer, cluster_transfer=cluster_transfer, couple_one=couple_one, pairs_one=pairs_one, count_one=count_one, couple_two=couple_two, pairs_two=pairs_two, count_two=count_two, near_blocks=near_blocks, near_list=near_list)


def couple_level(coeffs, partner_ids, counts, coupling):
    highest = lax.Precision.HIGHEST
    clusters = counts.shape[0]
    slot_index = jnp.arange(COUPLE_SLOTS, dtype=jnp.int32)[None, :]
    valid = (slot_index < counts[:, None]).astype(jnp.float32).reshape(-1)
    partner = jnp.take(coeffs, partner_ids, axis=0) * valid[:, None, None]
    terms = jnp.einsum("krs,ksp->krp", coupling, partner, precision=highest)
    return terms.reshape(clusters, COUPLE_SLOTS, terms.shape[1], terms.shape[2]).sum(1)


def reference(probes, leaf_basis, leaf_transfer, cluster_transfer, couple_one, pairs_one, count_one, couple_two, pairs_two, count_two, near_blocks, near_list):
    highest = lax.Precision.HIGHEST
    leaf_total, leaf_size, rank_size = leaf_basis.shape
    width = probes.shape[1]
    blocks = probes.reshape(leaf_total, leaf_size, width)
    leaf_coef = jnp.einsum("lnr,lnp->lrp", leaf_basis, blocks, precision=highest)
    coef_one = jnp.einsum("lrs,lrp->lsp", leaf_transfer, leaf_coef, precision=highest)
    coef_one = coef_one.reshape(-1, 4, rank_size, width).sum(1)
    coef_two = jnp.einsum("crs,crp->csp", cluster_transfer, coef_one, precision=highest)
    coef_two = coef_two.reshape(-1, 4, rank_size, width).sum(1)
    far_one = couple_level(coef_one, pairs_one, count_one, couple_one)
    far_two = couple_level(coef_two, pairs_two, count_two, couple_two)
    down_one = far_one + jnp.einsum("crs,csp->crp", cluster_transfer, jnp.repeat(far_two, 4, axis=0), precision=highest)
    child = jnp.einsum("lrs,lsp->lrp", leaf_transfer, jnp.repeat(down_one, 4, axis=0), precision=highest)
    far_rows = jnp.einsum("lnr,lrp->lnp", leaf_basis, child, precision=highest)

    def near_leaf(item):
        leaf_blocks, leaf_ids = item
        rows = jnp.take(blocks, leaf_ids, axis=0)
        return jnp.einsum("mab,mbp->ap", leaf_blocks, rows, precision=highest)

    near_rows = lax.map(near_leaf, (near_blocks, near_list))
    return (far_rows + near_rows).reshape(-1, width)
```

```python
import functools

import jax
import jax.numpy as jnp
from jax import lax
from jax.experimental import pallas as pl
from jax.experimental.pallas import tpu as pltpu
from jax.sharding import PartitionSpec as P

HIGH = lax.Precision.HIGH
LANES = 128
SIDE = 4
CHUNKS = ((0, 1), (1, 1), (2, 2), (4, 2), (6, 2))


def permuted(shard, target):
    pairs = []
    for i in range(lax.axis_size("leaf")):
        x, y, z, core = i // 32, i // 8 % 4, i // 2 % 4, i % 2
        to = target(x, y, z, core)
        if to is not None:
            pairs.append((i, ((to[0] * 4 + to[1]) * 4 + to[2]) * 2 + to[3]))
    return lax.ppermute(shard, "leaf", pairs)


def chip_swap(shard):
    return permuted(shard, lambda x, y, z, core: (x, y, z, 1 - core))


def along_z(shard, by):
    return permuted(shard, lambda x, y, z, core: (x, y, (z + by) % 4, core))


def along_y(shard, by):
    return permuted(shard, lambda x, y, z, core: (x, (y + by) % 4, z, core))


def along_x(shard, by):
    return permuted(
        shard, lambda x, y, z, core: (x + by, y, z, core) if 0 <= x + by < 4 else None
    )


def next_line(shard, by):
    peers = lax.axis_size("leaf")
    pairs = [(i, i + 8 * by) for i in range(peers) if 0 <= i + 8 * by < peers]
    return lax.ppermute(shard, "leaf", pairs)


def across_chips(shard):
    peers = lax.axis_size("leaf")
    pairs = [(i, i + 1 if i % 2 else i - 1) for i in range(1, peers - 1)]
    return lax.ppermute(shard, "leaf", pairs)


def split(value):
    high = value.astype(jnp.bfloat16)
    low = (value - high.astype(jnp.float32)).astype(jnp.bfloat16)
    return high, low


def dot(a, b):
    return jnp.dot(a, b, preferred_element_type=jnp.float32)


def dot3(a, b):
    a_high, a_low = split(a)
    b_high, b_low = split(b)
    return dot(a_high, b_high) + (dot(a_high, b_low) + dot(a_low, b_high))


def far_kernel(index, one, two, own, other, transfer, down):
    tables = (own, other)

    def term(table, row, slot, base):
        keep = index[base + 1, slot].astype(jnp.float32)
        return table[index[base, slot]] * keep

    far_two = jnp.zeros((64, LANES), jnp.float32)
    for side in range(2):
        for half in range(2):
            left = jnp.concatenate(
                [tables[side][2 * half + i, 2][:, :64] for i in range(2)], axis=1
            )
            right = jnp.concatenate(
                [term(two, None, side * 4 + 2 * half + i, 2) for i in range(2)], axis=0
            )
            far_two += dot3(left, right)
    for j in range(SIDE):
        total = dot3(transfer[j], far_two)
        for side in range(2):
            left = jnp.concatenate([tables[side][j, 0], tables[side][j, 1]], axis=1)
            right = jnp.concatenate(
                [term(one, None, side * 16 + j * 4 + s, 0) for s in range(4)], axis=0
            )
            total += dot3(left, right)
        down[j] = total


def far_field(index, one, two, own, other, transfer):
    vmem = pl.BlockSpec(memory_space=pltpu.VMEM)
    return pl.pallas_call(
        far_kernel,
        out_shape=jax.ShapeDtypeStruct((SIDE, 64, LANES), jnp.float32),
        in_specs=[pl.BlockSpec(memory_space=pltpu.SMEM)] + [vmem] * 5,
        out_specs=vmem,
        cost_estimate=pl.CostEstimate(
            flops=120_000_000, bytes_accessed=2_000_000, transcendentals=0
        ),
        name="far_field",
    )(index, one, two, own, other, transfer)


def near_kernel(width, where, blocks, mine, chip, cross, wide, *rest):
    downs, out, high, low = rest[:width], rest[-3], rest[-2], rest[-1]
    leaf, m = pl.program_id(0), pl.program_id(1)

    @pl.when((leaf == 0) & (m == 0))
    def _():
        for source, ref in enumerate((mine, chip, cross)):
            for i in range(2):
                a, b = split(ref[pl.ds(i * 512, 512), :])
                high[2 * source + i] = a
                low[2 * source + i] = b

    slot = where[leaf * 3 + m]
    a_high, a_low = split(blocks[0, 0])
    b_high = high[slot]
    b_low = low[slot]
    total = dot(a_high, b_high) + (dot(a_high, b_low) + dot(a_low, b_high))

    @pl.when(m == 0)
    def _():
        far = [dot3(wide[...], ref[0]) for ref in downs]
        out[...] = total + (jnp.concatenate(far, axis=1) if width > 1 else far[0])

    @pl.when(m > 0)
    def _():
        out[...] += total


def near_field(first, width, where, blocks, mine, chip, cross, wide, downs, out):
    cols = width * LANES
    at = first // width
    whole = pl.BlockSpec((1024, cols), lambda l, m, w: (0, at))
    in_specs = [
        pl.BlockSpec((1, 1, 512, 512), lambda l, m, w: (l, m, 0, 0)),
        whole,
        whole,
        pl.BlockSpec((1024, cols), lambda l, m, w: (0, 0)),
        pl.BlockSpec((512, 64), lambda l, m, w: (l, 0)),
    ]
    for unit in range(first, first + width):
        in_specs.append(
            pl.BlockSpec((1, 64, LANES), lambda l, m, w, unit=unit: (w[6 + unit], 0, 0))
        )
    args = [where, blocks, mine, chip, cross, wide] + [downs] * width
    aliases = {}
    if out is not None:
        in_specs.append(pl.BlockSpec(memory_space=pl.ANY))
        aliases = {len(args): 0}
        args.append(out)
    return pl.pallas_call(
        functools.partial(near_kernel, width),
        out_shape=jax.ShapeDtypeStruct((1024, 1024), jnp.float32),
        grid_spec=pltpu.PrefetchScalarGridSpec(
            num_scalar_prefetch=1,
            grid=(2, 3),
            in_specs=in_specs,
            out_specs=pl.BlockSpec((512, cols), lambda l, m, w: (l, at)),
            scratch_shapes=[
                pltpu.VMEM((6, 512, cols), jnp.bfloat16),
                pltpu.VMEM((6, 512, cols), jnp.bfloat16),
            ],
        ),
        input_output_aliases=aliases,
        compiler_params=pltpu.CompilerParams(
            dimension_semantics=("arbitrary", "arbitrary")
        ),
        cost_estimate=pl.CostEstimate(
            flops=3_600_000_000 * width // 3,
            bytes_accessed=8_000_000,
            transcendentals=0,
        ),
        name="near_field",
    )(*args)


def body(
    probes,
    leaf_basis,
    leaf_transfer,
    cluster_transfer,
    couple_one,
    pairs_one,
    count_one,
    couple_two,
    pairs_two,
    count_two,
    near_blocks,
    near_list,
):
    device = lax.axis_index("leaf")
    core, z = device % 2, device // 2 % 4
    line = device // 8
    y, x = line % 4, line // 4
    around = jnp.arange(4, dtype=jnp.int32)

    crosses = [
        across_chips(probes[:, first * LANES : (first + width) * LANES])
        for first, width in CHUNKS
    ]

    partners = jnp.concatenate([pairs_one, pairs_two]).astype(jnp.float32)
    partners = jnp.pad(partners[None, :], ((0, 63), (0, 59)))
    couplings = jnp.stack(
        [
            jnp.concatenate([couple_one[0], couple_one[1]], axis=1),
            jnp.concatenate([couple_one[2], couple_one[3]], axis=1),
            jnp.concatenate([couple_two[0], partners], axis=1),
        ]
    )
    own_table = jnp.stack(
        [
            couplings,
            along_z(couplings, -1),
            along_z(couplings, 2),
            along_z(couplings, 1),
        ]
    )
    other_table = chip_swap(own_table)

    wide = jnp.einsum("lnr,lrs->lns", leaf_basis, leaf_transfer, precision=HIGH)
    wide = wide.reshape(1024, 64)
    part = lax.dot_general(wide, probes, (((0,), (0,)), ((), ())), precision=HIGH)
    theirs = lax.dynamic_slice_in_dim(part, (1 - core) * 512, 512, axis=1)
    mine = lax.dynamic_slice_in_dim(part, core * 512, 512, axis=1)
    mine = mine + chip_swap(theirs)

    def columns(offset):
        return lax.dynamic_slice_in_dim(mine, (z + offset) % 4 * LANES, LANES, axis=1)

    level_one = jnp.stack(
        [
            columns(0),
            along_z(columns(3), -1),
            along_z(columns(2), 2),
            along_z(columns(1), 1),
        ]
    )
    transfer = jnp.take(cluster_transfer, line * 4 + (z + around) % 4, axis=0)
    coef_two = jnp.einsum("jrs,jrp->sp", transfer, level_one, precision=HIGH)
    chip = chip_swap(probes)

    plane = jnp.stack(
        [
            coef_two,
            along_y(coef_two, -1),
            along_y(coef_two, 2),
            along_y(coef_two, 1),
        ]
    )
    all_one = jnp.concatenate([next_line(level_one, 1), level_one, next_line(level_one, -1)])
    all_two = jnp.concatenate([along_x(plane, 1), plane, along_x(plane, -1)])

    ids = jnp.stack([own_table[:, 2, 0, 64:69], other_table[:, 2, 0, 64:69]])
    ids = ids.astype(jnp.int32)
    cores = jnp.stack([core, 1 - core])
    cluster = line * 4 + (z + around) % 4
    slot_one = cores[:, None, None] * 4 + around[None, None, :]
    keep_one = slot_one < jnp.take(count_one, cluster)[None, :, None]
    id_one = ids[:, :, :4]
    at_one = (id_one // 4 - line + 1) * 4 + (id_one % 4 - z) % 4
    slot_two = (z + around)[None, :] % 4 * 2 + cores[:, None]
    keep_two = slot_two < count_two[line]
    id_two = ids[:, :, 4]
    at_two = (id_two // 4 - x + 1) * 4 + (id_two % 4 - y) % 4
    pad = ((0, 0), (0, 24))
    index = jnp.concatenate(
        [
            jnp.clip(at_one, 0, 11).reshape(1, 32),
            keep_one.astype(jnp.int32).reshape(1, 32),
            jnp.pad(jnp.clip(at_two, 0, 11).reshape(1, 8), pad),
            jnp.pad(keep_two.astype(jnp.int32).reshape(1, 8), pad),
        ]
    )

    down = far_field(index, all_one, all_two, own_table, other_table, transfer)
    back = jnp.stack(
        [down[0], along_z(down[3], -1), along_z(down[2], 2), along_z(down[1], 1)]
    )
    downs = jnp.concatenate([back, chip_swap(back)])

    local = near_list.reshape(-1) - 2 * device
    before = jnp.where(core == 0, 4, 2) + local + 2
    after = jnp.where(core == 0, 2, 4) + local - 2
    source = jnp.where(local < 0, before, jnp.where(local > 1, after, local))
    units = jnp.arange(8, dtype=jnp.int32)
    unit_at = jnp.where(units // 4 == core, 0, 4) + (units % 4 - z) % 4
    where = jnp.concatenate([source, unit_at]).astype(jnp.int32)
    out = None
    for (first, width), cross in zip(CHUNKS, crosses):
        out = near_field(
            first, width, where, near_blocks, probes, chip, cross, wide, downs, out
        )
    return out


def solution(mesh):
    return jax.shard_map(
        body,
        mesh=mesh,
        in_specs=(
            P("leaf", None),
            P("leaf", None, None),
            P("leaf", None, None),
            P(),
            P("leaf", None, None),
            P("leaf"),
            P(),
            P("leaf", None, None),
            P("leaf"),
            P(),
            P("leaf", None, None, None),
            P("leaf", None),
        ),
        out_specs=P("leaf", None),
        check_vma=False,
    )
```

```python
import functools

import jax
import jax.numpy as jnp
from jax import lax
from jax.experimental import pallas as pl
from jax.experimental.pallas import tpu as pltpu
from jax.sharding import PartitionSpec as P


LANES = 128
SIDE = 4
CHUNKS = ((0, 3), (3, 2), (5, 3))
RINGS = 2


def permuted(shard, target):
    pairs = []
    for i in range(lax.axis_size("leaf")):
        x, y, z, core = i // 32, i // 8 % 4, i // 2 % 4, i % 2
        to = target(x, y, z, core)
        if to is not None:
            pairs.append((i, ((to[0] * 4 + to[1]) * 4 + to[2]) * 2 + to[3]))
    return lax.ppermute(shard, "leaf", pairs)


def chip_swap(shard):
    return permuted(shard, lambda x, y, z, core: (x, y, z, 1 - core))


def along_z(shard, by):
    return permuted(shard, lambda x, y, z, core: (x, y, (z + by) % 4, core))


def along_y(shard, by):
    return permuted(shard, lambda x, y, z, core: (x, (y + by) % 4, z, core))


def along_x(shard, by):
    return permuted(
        shard, lambda x, y, z, core: (x + by, y, z, core) if 0 <= x + by < 4 else None
    )


def across_chips(shard):
    peers = lax.axis_size("leaf")
    pairs = [(i, i + 1 if i % 2 else i - 1) for i in range(1, peers - 1)]
    return lax.ppermute(shard, "leaf", pairs)


def round_line(shard):
    return permuted(
        shard,
        lambda x, y, z, core: (x, y, (z + 1) % 4, 0) if core else (x, y, (z - 1) % 4, 1),
    )


def relayed(shard):
    pairs = [(i, i + 8) for i in range(0, lax.axis_size("leaf") - 8, 8)]
    pairs += [(i + 15, i + 7) for i, _ in pairs]
    return lax.ppermute(shard, "leaf", pairs)


def ahead(shard):
    return permuted(shard, lambda x, y, z, core: (x, y, (z + 1 - 2 * core) % 4, core))


def opposite(shard):
    return permuted(
        shard, lambda x, y, z, core: (x, y, (z + 2) % 4, core) if core == z % 2 else None
    )


def split(value):
    high = value.astype(jnp.bfloat16)
    low = (value - high.astype(jnp.float32)).astype(jnp.bfloat16)
    return high, low


def dot(a, b):
    return jnp.dot(a, b, preferred_element_type=jnp.float32)


def dot3(a, b):
    a_high, a_low = split(a)
    b_high, b_low = split(b)
    return dot(a_high, b_high) + (dot(a_high, b_low) + dot(a_low, b_high))


VMEM = pl.BlockSpec(memory_space=pltpu.VMEM)
ANY = pl.BlockSpec(memory_space=pl.ANY)
SMEM = pl.BlockSpec(memory_space=pltpu.SMEM)
HBM = pl.BlockSpec(memory_space=pltpu.HBM)
F32 = jnp.float32


def shape(*dims, dtype=F32):
    return jax.ShapeDtypeStruct(dims, dtype)


def place(device):
    number = device[0]
    line = number // 8
    return number % 2, number // 2 % 4, line, line % 4, line // 4


def leaf_kernel(
    device, pairs_one, pairs_two, probes, basis, transfer, couple_one, couple_two, clusters,
    mine, theirs, couplings, around, wide, high, low, *rest,
):
    slices, (basis_in, transfer_in, couple_in, part, sems, small) = rest[:-6], rest[-6:]
    core, z, line, _, _ = place(device)

    def start(source, target, sem):
        copy = pltpu.make_async_copy(source, target, sem)
        copy.start()
        return copy

    little = [start(basis, basis_in, small.at[0]), start(transfer, transfer_in, small.at[1])]
    copies = []
    for (at, width), ref, i in zip(CHUNKS, slices, range(len(CHUNKS))):
        source = probes.at[:, pl.ds(at * LANES, width * LANES)]
        copies.append(start(source, ref, sems.at[i]))
    later = [
        start(couple_one, couple_in.at[pl.ds(0, 4)], small.at[2]),
        start(couple_two, couple_in.at[pl.ds(4, 1)], small.at[3]),
    ]
    for j in range(SIDE):
        cluster = line * 4 + (z + j) % 4
        later.append(start(clusters.at[cluster], around.at[j], small.at[4 + j]))
    for copy in little:
        copy.wait()
    rows = [dot3(transfer_in[leaf].T, basis_in[leaf]) for leaf in range(2)]
    across = jnp.concatenate(rows, axis=1)
    w_high, w_low = split(across.T)
    wide[...] = jnp.concatenate([w_high, w_low, w_high], axis=1)
    w_high, w_low = split(across)
    w_both = jnp.concatenate([w_high, w_low], axis=0)
    for copy in later:
        copy.wait()
    couplings[0] = jnp.concatenate([couple_in[0], couple_in[1]], axis=1)
    couplings[1] = jnp.concatenate([couple_in[2], couple_in[3]], axis=1)
    lane = lax.broadcasted_iota(jnp.int32, (64, 64), 1)
    ids = jnp.zeros((64, 64), F32)
    for i in range(5):
        value = pairs_one[i] if i < 4 else pairs_two[0]
        ids = jnp.where(lane == i, value.astype(F32), ids)
    couplings[2] = jnp.concatenate([couple_in[4], ids], axis=1)
    for (at, width), ref, copy in zip(CHUNKS, slices, copies):
        copy.wait()
        cols = pl.ds(at * LANES, width * LANES)
        a, b = split(ref[...])
        high[:, cols] = a
        low[:, cols] = b
        terms = dot(w_both, a)
        part[:, cols] = terms[:64] + (terms[64:] + dot(w_high, b))
    mine[...] = part[:, pl.ds(pl.multiple_of(core * 512, 512), 512)]
    theirs[...] = part[:, pl.ds(pl.multiple_of((1 - core) * 512, 512), 512)]


def leaf_stage(device, pairs_one, pairs_two, *arrays):
    bf16 = jnp.bfloat16
    shapes = [shape(64, 512), shape(64, 512), shape(3, 64, LANES), shape(4, 64, 64)]
    shapes += [shape(1024, 192, dtype=bf16), shape(1024, 1024, dtype=bf16), shape(1024, 1024, dtype=bf16)]
    shapes += [shape(1024, width * LANES) for _, width in CHUNKS]
    return pl.pallas_call(
        leaf_kernel,
        out_shape=shapes,
        in_specs=[SMEM] * 3 + [HBM] * 6,
        out_specs=[VMEM] * len(shapes),
        scratch_shapes=[
            pltpu.VMEM((2, 64, 512), F32),
            pltpu.VMEM((2, 64, 64), F32),
            pltpu.VMEM((5, 64, 64), F32),
            pltpu.VMEM((64, 1024), F32),
            pltpu.SemaphoreType.DMA((len(CHUNKS),)),
            pltpu.SemaphoreType.DMA((8,)),
        ],
        compiler_params=pltpu.CompilerParams(vmem_limit_bytes=12 << 20),
        cost_estimate=pl.CostEstimate(
            flops=400_000_000, bytes_accessed=8_000_000, transcendentals=0
        ),
        name="leaf_stage",
    )(
        device,
        pairs_one,
        pairs_two,
        *[pltpu.with_memory_space_constraint(a, pltpu.HBM) for a in arrays],
    )


def small_call(kernel, outs, *args, scalars=1, scratch=()):
    return pl.pallas_call(
        kernel,
        out_shape=outs,
        in_specs=[SMEM] * scalars + [VMEM] * (len(args) - scalars),
        out_specs=[VMEM] * len(outs),
        scratch_shapes=list(scratch),
        compiler_params=pltpu.CompilerParams(vmem_limit_bytes=10 << 20),
        cost_estimate=pl.CostEstimate(
            flops=10_000_000, bytes_accessed=1_000_000, transcendentals=0
        ),
    )(*args)


def cut_kernel(device, mine, got, *pieces):
    _, z, _, _, _ = place(device)
    for j, piece in enumerate(pieces):
        cols = pl.ds(pl.multiple_of((z + j) % 4 * LANES, LANES), LANES)
        piece[...] = mine[:, cols] + got[:, cols]


def lift_kernel(device, first, second, third, fourth, around, level, coef):
    total = jnp.zeros((64, LANES), F32)
    for j, ref in enumerate((first, second, third, fourth)):
        value = ref[...]
        level[j] = value
        total += dot3(around[j].T, value)
    level[4] = total
    coef[...] = total


def plane_kernel(device, level, below, across, above, plane, from_below, from_above):
    plane[0] = level[4]
    plane[1] = above[4]
    plane[2] = across[...]
    plane[3] = below[4]
    for target, source in ((from_below, below), (from_above, above)):
        target[pl.ds(0, 4)] = plane[...]
        target[pl.ds(4, 4)] = source[pl.ds(0, 4)]


def far_kernel(device, count_one, count_two, *refs):
    level, below, above, plane, before, after, own, other, around = refs[:9]
    down, one, two, ids, sems = refs[9:]
    core, z, line, y, x = place(device)
    tables = (own, other)
    copies = []
    for side in range(2):
        for j in range(SIDE):
            i = side * 4 + j
            source = tables[side].at[j, 2, pl.ds(0, 8), :]
            copies.append(pltpu.make_async_copy(source, ids.at[i], sems.at[i]))
            copies[-1].start()
    one[pl.ds(4, 4)] = level[pl.ds(0, 4)]
    one[pl.ds(0, 4)] = jnp.where(y == 0, before[pl.ds(4, 4)], below[pl.ds(0, 4)])
    one[pl.ds(8, 4)] = jnp.where(y == 3, after[pl.ds(4, 4)], above[pl.ds(0, 4)])
    two[pl.ds(0, 4)] = before[pl.ds(0, 4)]
    two[pl.ds(4, 4)] = plane[...]
    two[pl.ds(8, 4)] = after[pl.ds(0, 4)]
    for copy in copies:
        copy.wait()

    def partner(side, j, s):
        return ids[side * 4 + j, 0, 64 + s].astype(jnp.int32)

    def kept(value, keep):
        return jnp.where(keep, value, jnp.zeros_like(value))

    far_two = jnp.zeros((64, LANES), F32)
    for side in range(2):
        left, right = [], []
        for j in range(SIDE):
            left.append(tables[side][j, 2][:, :64])
            p = partner(side, j, 4)
            slot = (z + j) % 4 * 2 + (core if side == 0 else 1 - core)
            at = jnp.clip((p // 4 - x + 1) * 4 + (p % 4 - y + 4) % 4, 0, 11)
            right.append(kept(two[at], slot < count_two[line]))
        far_two += dot3(jnp.concatenate(left, axis=1), jnp.concatenate(right, axis=0))
    for j in range(SIDE):
        total = dot3(around[j], far_two)
        count = count_one[line * 4 + (z + j) % 4]
        for side in range(2):
            left = jnp.concatenate([tables[side][j, 0], tables[side][j, 1]], axis=1)
            right = []
            for s in range(4):
                p = partner(side, j, s)
                slot = (core if side == 0 else 1 - core) * 4 + s
                at = jnp.clip((p // 4 - line + 1) * 4 + (p % 4 - z + 4) % 4, 0, 11)
                right.append(kept(one[at], slot < count))
            total += dot3(left, jnp.concatenate(right, axis=0))
        down[j] = total


def pack_kernel(device, down, other, first, second):
    core, _, _, _, _ = place(device)
    for side in range(2):
        for target, j in ((first, 1 + 2 * core), (second, 2)):
            target[side] = jnp.where(core == side, down[j], other[j])


def unpack_kernel(device, down, other, back, other_back, table):
    core, z, _, _, _ = place(device)

    def got(on, kind, side):
        return jnp.where(core == on, back[kind, side], other_back[kind, side])

    def put(side, chip, value):
        cols = pl.ds(pl.multiple_of((side * 4 + chip) * LANES, LANES), LANES)
        high, low = split(value)
        table[:, cols] = jnp.concatenate([high, high, low], axis=0)

    for side in range(2):
        put(side, z, jnp.where(core == side, down[0], other[0]))
        put(side, (z + 1) % 4, got(1, 0, side))
        put(side, (z + 2) % 4, got(z % 2, 1, side))
        put(side, (z + 3) % 4, got(0, 0, side))


def block_kernel(blocks, high, low):
    for i in range(6):
        high[i], low[i] = split(blocks[i // 3, i % 3])


def block_stage(near_blocks):
    half = shape(6, 512, 512, dtype=jnp.bfloat16)
    return small_call(block_kernel, [half, half], near_blocks, scalars=0)


def near_kernel(at, width, at_old, last, device, near_list, *refs):
    n_high, n_low, p_high, p_low, chip, wide, table, cross, relay = refs[:9]
    both, sems = refs[-2:]
    old = (at_old, refs[9]) if at_old is not None else None
    if last:
        out, buffer = refs[-4], refs[-3]
    else:
        out, buffer = (refs[-4] if old else None), refs[-3]
    core, z, _, _, _ = place(device)
    span = width * LANES
    cols = pl.ds(at * LANES, span)
    high, low = pl.ds(0, span), pl.ds(span, span)
    for i in range(2):
        rows = pl.ds(i * 512, 512)
        both[i, :, high], both[i, :, low] = p_high[rows, cols], p_low[rows, cols]
        both[2 + i, :, high], both[2 + i, :, low] = split(chip[rows, cols])
        beside = cross[rows, :]
        if at < CHUNKS[RINGS][0]:
            beside = jnp.where(z == 3 * core, relay[rows, :], beside)
        both[4 + i, :, high], both[4 + i, :, low] = split(beside)
    copies = []
    if old:
        (at_old, buffer_old) = old
        copies.append(
            pltpu.make_async_copy(
                buffer_old, out.at[:, pl.ds(at_old * LANES, buffer_old.shape[1])], sems.at[2]
            )
        )
        copies[-1].start()
    for leaf in range(2):
        rows = pl.ds(leaf * 512, 512)
        total = dot(wide[rows, :], table[:, cols])
        for m in range(3):
            i = leaf * 3 + m
            local = near_list[leaf, m] - 2 * device[0]
            before = jnp.where(core == 0, 4, 2) + local + 2
            after = jnp.where(core == 0, 2, 4) + local - 2
            slot = jnp.where(local < 0, before, jnp.where(local > 1, after, local))
            wide_terms = dot(n_high[i], both[slot])
            total += wide_terms[:, :span]
            total += wide_terms[:, span:]
            total += dot(n_low[i], both[slot, :, high])
        buffer[rows, :] = total
        if last:
            copies.append(
                pltpu.make_async_copy(buffer.at[rows], out.at[rows, cols], sems.at[leaf])
            )
            copies[-1].start()
    for copy in copies:
        copy.wait()


def near_field(chunk, device, near_list, arrays, old, out):
    (at, width), last = CHUNKS[chunk], chunk == len(CHUNKS) - 1
    cols = width * LANES
    at_old = CHUNKS[chunk - 1][0] if chunk else None
    args = [device, near_list, *arrays]
    in_specs = [SMEM] * 2 + [VMEM] * len(arrays)
    aliases = {}
    if chunk:
        args.append(old)
        in_specs.append(VMEM)
    if out is not None:
        in_specs.append(ANY)
        aliases = {len(args): 0}
        args.append(out)
    shapes, out_specs = [], []
    if chunk:
        shapes.append(shape(1024, 1024))
        out_specs.append(ANY)
    scratch = []
    if last:
        scratch.append(pltpu.VMEM((1024, cols), F32))
    else:
        shapes.append(shape(1024, cols))
        out_specs.append(VMEM)
    scratch.append(pltpu.VMEM((6, 512, 2 * cols), jnp.bfloat16))
    scratch.append(pltpu.SemaphoreType.DMA((3,)))
    results = pl.pallas_call(
        functools.partial(near_kernel, at, width, at_old, last),
        out_shape=shapes,
        in_specs=in_specs,
        out_specs=out_specs,
        scratch_shapes=scratch,
        input_output_aliases=aliases,
        compiler_params=pltpu.CompilerParams(vmem_limit_bytes=16 << 20),
        cost_estimate=pl.CostEstimate(
            flops=1_250_000_000 * width, bytes_accessed=2_000_000, transcendentals=0
        ),
        name="near_field",
    )(*args)
    return (results[0] if chunk else None), (None if last else results[-1])


def body(
    probes,
    leaf_basis,
    leaf_transfer,
    cluster_transfer,
    couple_one,
    pairs_one,
    count_one,
    couple_two,
    pairs_two,
    count_two,
    near_blocks,
    near_list,
):
    device = lax.axis_index("leaf").reshape(1)

    mine, theirs, couplings, around, wide, p_high, p_low, *slices = leaf_stage(
        device,
        pairs_one,
        pairs_two,
        probes,
        jnp.swapaxes(leaf_basis, 1, 2),
        leaf_transfer,
        couple_one,
        couple_two,
        cluster_transfer,
    )
    crosses, relays = [], []
    for i, piece in enumerate(slices):
        if i < RINGS:
            crosses.append(round_line(piece))
            relays.append(relayed(crosses[i]))
        else:
            crosses.append(across_chips(piece))
            relays.append(crosses[i])

    own_table = jnp.stack(
        [
            couplings,
            along_z(couplings, -1),
            along_z(couplings, 2),
            along_z(couplings, 1),
        ]
    )
    other_table = chip_swap(own_table)

    got = chip_swap(theirs)
    pieces = small_call(cut_kernel, [shape(64, LANES)] * 4, device, mine, got)
    level, coef_two = small_call(
        lift_kernel,
        [shape(5, 64, LANES), shape(64, LANES)],
        device,
        pieces[0],
        along_z(pieces[3], -1),
        along_z(pieces[2], 2),
        along_z(pieces[1], 1),
        around,
    )
    chip = chip_swap(probes)
    blocks = block_stage(near_blocks)

    above = along_y(level, -1)
    across = along_y(coef_two, 2)
    below = along_y(level, 1)
    plane, upward, downward = small_call(
        plane_kernel,
        [shape(4, 64, LANES), shape(8, 64, LANES), shape(8, 64, LANES)],
        device,
        level,
        below,
        across,
        above,
    )
    (down,) = small_call(
        far_kernel,
        [shape(4, 64, LANES)],
        device,
        count_one,
        count_two,
        level,
        below,
        above,
        plane,
        along_x(upward, 1),
        along_x(downward, -1),
        own_table,
        other_table,
        around,
        scalars=3,
        scratch=(
            pltpu.VMEM((12, 64, LANES), F32),
            pltpu.VMEM((12, 64, LANES), F32),
            pltpu.SMEM((8, 8, LANES), F32),
            pltpu.SemaphoreType.DMA((8,)),
        ),
    )
    other = chip_swap(down)
    pair = [shape(2, 64, LANES)] * 2
    first, second = small_call(pack_kernel, pair, device, down, other)
    back = jnp.stack([ahead(first), opposite(second)])
    other_back = chip_swap(back)
    (table,) = small_call(
        unpack_kernel, [shape(192, 1024, dtype=jnp.bfloat16)], device, down, other, back, other_back
    )

    out = old = None
    for i, (cross, relay) in enumerate(zip(crosses, relays)):
        arrays = (*blocks, p_high, p_low, chip, wide, table, cross, relay)
        out, old = near_field(i, device, near_list, arrays, old, out)
    return out


def solution(mesh):
    return jax.shard_map(
        body,
        mesh=mesh,
        in_specs=(
            P("leaf", None),
            P("leaf", None, None),
            P("leaf", None, None),
            P(),
            P("leaf", None, None),
            P("leaf"),
            P(),
            P("leaf", None, None),
            P("leaf"),
            P(),
            P("leaf", None, None, None),
            P("leaf", None),
        ),
        out_specs=P("leaf", None),
        check_vma=False,
    )
```

```python
import functools

import jax
import jax.numpy as jnp
from jax import lax
from jax.experimental import pallas as pl
from jax.experimental.pallas import tpu as pltpu
from jax.sharding import PartitionSpec as P


LANES = 128
SIDE = 4
CHUNKS = ((0, 3), (3, 2), (5, 3))
RINGS = 2


def permuted(shard, target):
    pairs = []
    for i in range(lax.axis_size("leaf")):
        x, y, z, core = i // 32, i // 8 % 4, i // 2 % 4, i % 2
        to = target(x, y, z, core)
        if to is not None:
            pairs.append((i, ((to[0] * 4 + to[1]) * 4 + to[2]) * 2 + to[3]))
    return lax.ppermute(shard, "leaf", pairs)


def chip_swap(shard):
    return permuted(shard, lambda x, y, z, core: (x, y, z, 1 - core))


def along_z(shard, by):
    return permuted(shard, lambda x, y, z, core: (x, y, (z + by) % 4, core))


def along_y(shard, by):
    return permuted(shard, lambda x, y, z, core: (x, (y + by) % 4, z, core))


def along_x(shard, by):
    return permuted(
        shard, lambda x, y, z, core: (x + by, y, z, core) if 0 <= x + by < 4 else None
    )


def across_chips(shard):
    peers = lax.axis_size("leaf")
    pairs = [(i, i + 1 if i % 2 else i - 1) for i in range(1, peers - 1)]
    return lax.ppermute(shard, "leaf", pairs)


def round_line(shard):
    return permuted(
        shard,
        lambda x, y, z, core: (x, y, (z + 1) % 4, 0) if core else (x, y, (z - 1) % 4, 1),
    )


def relayed(shard):
    pairs = [(i, i + 8) for i in range(0, lax.axis_size("leaf") - 8, 8)]
    pairs += [(i + 15, i + 7) for i, _ in pairs]
    return lax.ppermute(shard, "leaf", pairs)


def ahead(shard):
    return permuted(shard, lambda x, y, z, core: (x, y, (z + 1 - 2 * core) % 4, core))


def opposite(shard):
    return permuted(
        shard, lambda x, y, z, core: (x, y, (z + 2) % 4, core) if core == z % 2 else None
    )


def split(value):
    high = value.astype(jnp.bfloat16)
    low = (value - high.astype(jnp.float32)).astype(jnp.bfloat16)
    return high, low


def dot(a, b):
    return jnp.dot(a, b, preferred_element_type=jnp.float32)


def dot3(a, b):
    a_high, a_low = split(a)
    b_high, b_low = split(b)
    return dot(a_high, b_high) + (dot(a_high, b_low) + dot(a_low, b_high))


VMEM = pl.BlockSpec(memory_space=pltpu.VMEM)
ANY = pl.BlockSpec(memory_space=pl.ANY)
SMEM = pl.BlockSpec(memory_space=pltpu.SMEM)
HBM = pl.BlockSpec(memory_space=pltpu.HBM)
F32 = jnp.float32


def shape(*dims, dtype=F32):
    return jax.ShapeDtypeStruct(dims, dtype)


def place(device):
    number = device[0]
    line = number // 8
    return number % 2, number // 2 % 4, line, line % 4, line // 4


def leaf_kernel(
    device, pairs_one, pairs_two, probes, basis, transfer, couple_one, couple_two, clusters,
    mine, theirs, couplings, around, wide, high, low, *rest,
):
    slices, (basis_in, transfer_in, couple_in, part, sems, small) = rest[:-6], rest[-6:]
    core, z, line, _, _ = place(device)

    def start(source, target, sem):
        copy = pltpu.make_async_copy(source, target, sem)
        copy.start()
        return copy

    little = [start(basis, basis_in, small.at[0]), start(transfer, transfer_in, small.at[1])]
    copies = []
    for (at, width), ref, i in zip(CHUNKS, slices, range(len(CHUNKS))):
        source = probes.at[:, pl.ds(at * LANES, width * LANES)]
        copies.append(start(source, ref, sems.at[i]))
    later = [
        start(couple_one, couple_in.at[pl.ds(0, 4)], small.at[2]),
        start(couple_two, couple_in.at[pl.ds(4, 1)], small.at[3]),
    ]
    for j in range(SIDE):
        cluster = line * 4 + (z + j) % 4
        later.append(start(clusters.at[cluster], around.at[j], small.at[4 + j]))
    for copy in little:
        copy.wait()
    rows = [dot3(transfer_in[leaf].T, basis_in[leaf]) for leaf in range(2)]
    across = jnp.concatenate(rows, axis=1)
    w_high, w_low = split(across.T)
    wide[...] = jnp.concatenate([w_high, w_low, w_high], axis=1)
    w_high, w_low = split(across)
    w_both = jnp.concatenate([w_high, w_low], axis=0)
    for copy in later:
        copy.wait()
    couplings[0] = jnp.concatenate([couple_in[0], couple_in[1]], axis=1)
    couplings[1] = jnp.concatenate([couple_in[2], couple_in[3]], axis=1)
    lane = lax.broadcasted_iota(jnp.int32, (64, 64), 1)
    ids = jnp.zeros((64, 64), F32)
    for i in range(5):
        value = pairs_one[i] if i < 4 else pairs_two[0]
        ids = jnp.where(lane == i, value.astype(F32), ids)
    couplings[2] = jnp.concatenate([couple_in[4], ids], axis=1)
    for (at, width), ref, copy in zip(CHUNKS, slices, copies):
        copy.wait()
        cols = pl.ds(at * LANES, width * LANES)
        a, b = split(ref[...])
        high[:, cols] = a
        low[:, cols] = b
        terms = dot(w_both, a)
        part[:, cols] = terms[:64] + (terms[64:] + dot(w_high, b))
    mine[...] = part[:, pl.ds(pl.multiple_of(core * 512, 512), 512)]
    theirs[...] = part[:, pl.ds(pl.multiple_of((1 - core) * 512, 512), 512)]


def leaf_stage(device, pairs_one, pairs_two, *arrays):
    bf16 = jnp.bfloat16
    shapes = [shape(64, 512), shape(64, 512), shape(3, 64, LANES), shape(4, 64, 64)]
    shapes += [shape(1024, 192, dtype=bf16), shape(1024, 1024, dtype=bf16), shape(1024, 1024, dtype=bf16)]
    shapes += [shape(1024, width * LANES) for _, width in CHUNKS]
    return pl.pallas_call(
        leaf_kernel,
        out_shape=shapes,
        in_specs=[SMEM] * 3 + [HBM] * 6,
        out_specs=[VMEM] * len(shapes),
        scratch_shapes=[
            pltpu.VMEM((2, 64, 512), F32),
            pltpu.VMEM((2, 64, 64), F32),
            pltpu.VMEM((5, 64, 64), F32),
            pltpu.VMEM((64, 1024), F32),
            pltpu.SemaphoreType.DMA((len(CHUNKS),)),
            pltpu.SemaphoreType.DMA((8,)),
        ],
        compiler_params=pltpu.CompilerParams(vmem_limit_bytes=12 << 20),
        cost_estimate=pl.CostEstimate(
            flops=400_000_000, bytes_accessed=8_000_000, transcendentals=0
        ),
        name="leaf_stage",
    )(
        device,
        pairs_one,
        pairs_two,
        *[pltpu.with_memory_space_constraint(a, pltpu.HBM) for a in arrays],
    )


def small_call(kernel, outs, *args, scalars=1, scratch=()):
    return pl.pallas_call(
        kernel,
        out_shape=outs,
        in_specs=[SMEM] * scalars + [VMEM] * (len(args) - scalars),
        out_specs=[VMEM] * len(outs),
        scratch_shapes=list(scratch),
        compiler_params=pltpu.CompilerParams(vmem_limit_bytes=10 << 20),
        cost_estimate=pl.CostEstimate(
            flops=10_000_000, bytes_accessed=1_000_000, transcendentals=0
        ),
    )(*args)


def cut_kernel(device, mine, got, *pieces):
    _, z, _, _, _ = place(device)
    for j, piece in enumerate(pieces):
        cols = pl.ds(pl.multiple_of((z + j) % 4 * LANES, LANES), LANES)
        piece[...] = mine[:, cols] + got[:, cols]


def lift_kernel(device, first, second, third, fourth, around, level, coef):
    total = jnp.zeros((64, LANES), F32)
    for j, ref in enumerate((first, second, third, fourth)):
        value = ref[...]
        level[j] = value
        total += dot3(around[j].T, value)
    level[4] = total
    coef[...] = total


def plane_kernel(device, level, below, across, above, plane, from_below, from_above):
    plane[0] = level[4]
    plane[1] = above[4]
    plane[2] = across[...]
    plane[3] = below[4]
    for target, source in ((from_below, below), (from_above, above)):
        target[pl.ds(0, 4)] = plane[...]
        target[pl.ds(4, 4)] = source[pl.ds(0, 4)]


def far_kernel(device, count_one, count_two, *refs):
    level, below, above, plane, before, after, own, other, around = refs[:9]
    down, one, two, ids, sems = refs[9:]
    core, z, line, y, x = place(device)
    tables = (own, other)
    copies = []
    for side in range(2):
        for j in range(SIDE):
            i = side * 4 + j
            source = tables[side].at[j, 2, pl.ds(0, 8), :]
            copies.append(pltpu.make_async_copy(source, ids.at[i], sems.at[i]))
            copies[-1].start()
    one[pl.ds(4, 4)] = level[pl.ds(0, 4)]
    one[pl.ds(0, 4)] = jnp.where(y == 0, before[pl.ds(4, 4)], below[pl.ds(0, 4)])
    one[pl.ds(8, 4)] = jnp.where(y == 3, after[pl.ds(4, 4)], above[pl.ds(0, 4)])
    two[pl.ds(0, 4)] = before[pl.ds(0, 4)]
    two[pl.ds(4, 4)] = plane[...]
    two[pl.ds(8, 4)] = after[pl.ds(0, 4)]
    for copy in copies:
        copy.wait()

    def partner(side, j, s):
        return ids[side * 4 + j, 0, 64 + s].astype(jnp.int32)

    def kept(value, keep):
        return jnp.where(keep, value, jnp.zeros_like(value))

    far_two = jnp.zeros((64, LANES), F32)
    for side in range(2):
        left, right = [], []
        for j in range(SIDE):
            left.append(tables[side][j, 2][:, :64])
            p = partner(side, j, 4)
            slot = (z + j) % 4 * 2 + (core if side == 0 else 1 - core)
            at = jnp.clip((p // 4 - x + 1) * 4 + (p % 4 - y + 4) % 4, 0, 11)
            right.append(kept(two[at], slot < count_two[line]))
        far_two += dot3(jnp.concatenate(left, axis=1), jnp.concatenate(right, axis=0))
    for j in range(SIDE):
        total = dot3(around[j], far_two)
        count = count_one[line * 4 + (z + j) % 4]
        for side in range(2):
            left = jnp.concatenate([tables[side][j, 0], tables[side][j, 1]], axis=1)
            right = []
            for s in range(4):
                p = partner(side, j, s)
                slot = (core if side == 0 else 1 - core) * 4 + s
                at = jnp.clip((p // 4 - line + 1) * 4 + (p % 4 - z + 4) % 4, 0, 11)
                right.append(kept(one[at], slot < count))
            total += dot3(left, jnp.concatenate(right, axis=0))
        down[j] = total


def pack_kernel(device, down, other, first, second):
    core, _, _, _, _ = place(device)
    for side in range(2):
        for target, j in ((first, 1 + 2 * core), (second, 2)):
            target[side] = jnp.where(core == side, down[j], other[j])


def unpack_kernel(device, down, other, back, other_back, table):
    core, z, _, _, _ = place(device)

    def got(on, kind, side):
        return jnp.where(core == on, back[kind, side], other_back[kind, side])

    def put(side, chip, value):
        cols = pl.ds(pl.multiple_of((side * 4 + chip) * LANES, LANES), LANES)
        high, low = split(value)
        table[:, cols] = jnp.concatenate([high, high, low], axis=0)

    for side in range(2):
        put(side, z, jnp.where(core == side, down[0], other[0]))
        put(side, (z + 1) % 4, got(1, 0, side))
        put(side, (z + 2) % 4, got(z % 2, 1, side))
        put(side, (z + 3) % 4, got(0, 0, side))


def block_kernel(blocks, high, low):
    for i in range(6):
        high[i], low[i] = split(blocks[i // 3, i % 3])


def block_stage(near_blocks):
    half = shape(6, 512, 512, dtype=jnp.bfloat16)
    return small_call(block_kernel, [half, half], near_blocks, scalars=0)


def source_of(device, near_list, leaf, m):
    core = device[0] % 2
    local = near_list[leaf, m] - 2 * device[0]
    before = jnp.where(core == 0, 4, 2) + local + 2
    after = jnp.where(core == 0, 2, 4) + local - 2
    return jnp.where(local < 0, before, jnp.where(local > 1, after, local))


def add_product(buffer, rows, n_high, n_low, both, i, slot, span):
    terms = dot(n_high[i], both[slot])
    buffer[rows, :] += terms[:, :span] + (
        terms[:, span:] + dot(n_low[i], both[slot, :, pl.ds(0, span)])
    )


def early_kernel(at, width, device, near_list, *refs):
    n_high, n_low, p_high, p_low, chip, wide, table, buffer, both = refs
    span = width * LANES
    cols = pl.ds(at * LANES, span)
    high, low = pl.ds(0, span), pl.ds(span, span)
    for i in range(2):
        rows = pl.ds(i * 512, 512)
        both[i, :, high], both[i, :, low] = p_high[rows, cols], p_low[rows, cols]
        both[2 + i, :, high], both[2 + i, :, low] = split(chip[rows, cols])
    for leaf in range(2):
        rows = pl.ds(leaf * 512, 512)
        buffer[rows, :] = dot(wide[rows, :], table[:, cols])
        for m in range(3):
            slot = source_of(device, near_list, leaf, m)

            @pl.when(slot < 4)
            def _(leaf=leaf, m=m, rows=rows, slot=slot):
                add_product(buffer, rows, n_high, n_low, both, leaf * 3 + m, slot, span)


def near_early(device, near_list, arrays):
    at, width = CHUNKS[-1]
    cols = width * LANES
    (buffer,) = pl.pallas_call(
        functools.partial(early_kernel, at, width),
        out_shape=[shape(1024, cols)],
        in_specs=[SMEM] * 2 + [VMEM] * len(arrays),
        out_specs=[VMEM],
        scratch_shapes=[pltpu.VMEM((4, 512, 2 * cols), jnp.bfloat16)],
        compiler_params=pltpu.CompilerParams(vmem_limit_bytes=16 << 20),
        cost_estimate=pl.CostEstimate(
            flops=1_000_000_000 * width, bytes_accessed=2_000_000, transcendentals=0
        ),
        name="near_early",
    )(device, near_list, *arrays)
    return buffer


def near_kernel(at, width, at_old, last, device, near_list, *refs):
    n_high, n_low, p_high, p_low, chip, wide, table, cross, relay = refs[:9]
    both, sems = refs[-2:]
    old = (at_old, refs[9]) if at_old is not None else None
    if last:
        out, buffer = refs[-4], refs[-3]
    else:
        out, buffer = (refs[-4] if old else None), refs[-3]
    core, z, _, _, _ = place(device)
    span = width * LANES
    cols = pl.ds(at * LANES, span)
    high, low = pl.ds(0, span), pl.ds(span, span)
    for i in range(2):
        rows = pl.ds(i * 512, 512)
        if not last:
            both[i, :, high], both[i, :, low] = p_high[rows, cols], p_low[rows, cols]
            both[2 + i, :, high], both[2 + i, :, low] = split(chip[rows, cols])
        beside = cross[rows, :]
        if at < CHUNKS[RINGS][0]:
            beside = jnp.where(z == 3 * core, relay[rows, :], beside)
        both[4 + i, :, high], both[4 + i, :, low] = split(beside)
    copies = []
    if old:
        (at_old, buffer_old) = old
        copies.append(
            pltpu.make_async_copy(
                buffer_old, out.at[:, pl.ds(at_old * LANES, buffer_old.shape[1])], sems.at[2]
            )
        )
        copies[-1].start()
    for leaf in range(2):
        rows = pl.ds(leaf * 512, 512)
        if last:
            buffer[rows, :] = refs[10][rows, :]
            for m in range(3):
                slot = source_of(device, near_list, leaf, m)

                @pl.when(slot >= 4)
                def _(leaf=leaf, m=m, rows=rows, slot=slot):
                    add_product(buffer, rows, n_high, n_low, both, leaf * 3 + m, slot, span)
        else:
            total = dot(wide[rows, :], table[:, cols])
            for m in range(3):
                i = leaf * 3 + m
                slot = source_of(device, near_list, leaf, m)
                wide_terms = dot(n_high[i], both[slot])
                total += wide_terms[:, :span]
                total += wide_terms[:, span:]
                total += dot(n_low[i], both[slot, :, high])
            buffer[rows, :] = total
        if last:
            copies.append(
                pltpu.make_async_copy(buffer.at[rows], out.at[rows, cols], sems.at[leaf])
            )
            copies[-1].start()
    for copy in copies:
        copy.wait()


def near_field(chunk, device, near_list, arrays, old, early, out):
    (at, width), last = CHUNKS[chunk], chunk == len(CHUNKS) - 1
    cols = width * LANES
    at_old = CHUNKS[chunk - 1][0] if chunk else None
    args = [device, near_list, *arrays]
    in_specs = [SMEM] * 2 + [VMEM] * len(arrays)
    aliases = {}
    if chunk:
        args.append(old)
        in_specs.append(VMEM)
    if last:
        args.append(early)
        in_specs.append(VMEM)
    if out is not None:
        in_specs.append(ANY)
        aliases = {len(args): 0}
        args.append(out)
    shapes, out_specs = [], []
    if chunk:
        shapes.append(shape(1024, 1024))
        out_specs.append(ANY)
    scratch = []
    if last:
        scratch.append(pltpu.VMEM((1024, cols), F32))
    else:
        shapes.append(shape(1024, cols))
        out_specs.append(VMEM)
    scratch.append(pltpu.VMEM((6, 512, 2 * cols), jnp.bfloat16))
    scratch.append(pltpu.SemaphoreType.DMA((3,)))
    results = pl.pallas_call(
        functools.partial(near_kernel, at, width, at_old, last),
        out_shape=shapes,
        in_specs=in_specs,
        out_specs=out_specs,
        scratch_shapes=scratch,
        input_output_aliases=aliases,
        compiler_params=pltpu.CompilerParams(vmem_limit_bytes=16 << 20),
        cost_estimate=pl.CostEstimate(
            flops=1_250_000_000 * width, bytes_accessed=2_000_000, transcendentals=0
        ),
        name="near_field",
    )(*args)
    return (results[0] if chunk else None), (None if last else results[-1])


def body(
    probes,
    leaf_basis,
    leaf_transfer,
    cluster_transfer,
    couple_one,
    pairs_one,
    count_one,
    couple_two,
    pairs_two,
    count_two,
    near_blocks,
    near_list,
):
    device = lax.axis_index("leaf").reshape(1)

    mine, theirs, couplings, around, wide, p_high, p_low, *slices = leaf_stage(
        device,
        pairs_one,
        pairs_two,
        probes,
        jnp.swapaxes(leaf_basis, 1, 2),
        leaf_transfer,
        couple_one,
        couple_two,
        cluster_transfer,
    )
    crosses, relays = [], []
    for i, piece in enumerate(slices):
        if i < RINGS:
            crosses.append(round_line(piece))
            relays.append(relayed(crosses[i]))
        else:
            crosses.append(across_chips(piece))
            relays.append(crosses[i])

    own_table = jnp.stack(
        [couplings, along_z(couplings, -1), along_z(couplings, 2), along_z(couplings, 1)]
    )
    other_table = chip_swap(own_table)

    got = chip_swap(theirs)
    pieces = small_call(cut_kernel, [shape(64, LANES)] * 4, device, mine, got)
    level, coef_two = small_call(
        lift_kernel,
        [shape(5, 64, LANES), shape(64, LANES)],
        device,
        pieces[0],
        along_z(pieces[3], -1),
        along_z(pieces[2], 2),
        along_z(pieces[1], 1),
        around,
    )
    chip = chip_swap(probes)
    blocks = block_stage(near_blocks)

    above = along_y(level, -1)
    across = along_y(coef_two, 2)
    below = along_y(level, 1)
    plane, upward, downward = small_call(
        plane_kernel,
        [shape(4, 64, LANES), shape(8, 64, LANES), shape(8, 64, LANES)],
        device,
        level,
        below,
        across,
        above,
    )
    (down,) = small_call(
        far_kernel,
        [shape(4, 64, LANES)],
        device,
        count_one,
        count_two,
        level,
        below,
        above,
        plane,
        along_x(upward, 1),
        along_x(downward, -1),
        own_table,
        other_table,
        around,
        scalars=3,
        scratch=(
            pltpu.VMEM((12, 64, LANES), F32),
            pltpu.VMEM((12, 64, LANES), F32),
            pltpu.SMEM((8, 8, LANES), F32),
            pltpu.SemaphoreType.DMA((8,)),
        ),
    )
    other = chip_swap(down)
    pair = [shape(2, 64, LANES)] * 2
    first, second = small_call(pack_kernel, pair, device, down, other)
    back = jnp.stack([ahead(first), opposite(second)])
    other_back = chip_swap(back)
    (table,) = small_call(
        unpack_kernel, [shape(192, 1024, dtype=jnp.bfloat16)], device, down, other, back, other_back
    )

    local = (*blocks, p_high, p_low, chip, wide, table)
    early = near_early(device, near_list, local)
    out = old = None
    for i, (cross, relay) in enumerate(zip(crosses, relays)):
        arrays = (*blocks, p_high, p_low, chip, wide, table, cross, relay)
        out, old = near_field(i, device, near_list, arrays, old, early, out)
    return out


def solution(mesh):
    return jax.shard_map(
        body,
        mesh=mesh,
        in_specs=(
            P("leaf", None),
            P("leaf", None, None),
            P("leaf", None, None),
            P(),
            P("leaf", None, None),
            P("leaf"),
            P(),
            P("leaf", None, None),
            P("leaf"),
            P(),
            P("leaf", None, None, None),
            P("leaf", None),
        ),
        out_specs=P("leaf", None),
        check_vma=False,
    )
```
